256 devices in a mesh: space: 16 (over x_hi, z), tm: 16 (over y, x_lo, core).
Axes of the slice: x: 4 (x_hi: 2, x_lo: 2; x = x_hi * 2 + x_lo), y: 4, z: 8, core: 2. Of those that a mesh axis runs over, the one named last changes fastest.
Arguments:
- snapshots: bfloat16 [163840, 8192], P('space', 'tm'), may hold values from -6 to 6
- modes: bfloat16 [163840, 256], P('space'), may hold values from -0.015625 to 0.015625
Outputs:
- gram: float32 [4864, 4864], P('tm', 'space')
- rhs: float32 [4864, 256], P('tm', 'space')
The draws below stay inside these ranges and needn't reach their ends.
All inputs are finite; a program needn't handle non-finite values.
Results may differ from the reference program's by a relative error of at most 0.0057.
Values may be sent and summed in bfloat16 or wider, within the bound.
A program may use at most 128 MiB of HBM per device.

```python
import jax
import jax.numpy as jnp
from jax import lax

BASIS_MODES = 256
LEAD_MODES = 48
SNAP_DEV = 512
FEATURES = 4864
DELAY_GAP = 512
DOF_TOTAL = 163840
SNAPSHOTS = 8192
N_TM = 16


def block_levels(rng, extent, split, smallest, top_value):
    def one(axis_at, parts):
        steps = jax.random.uniform(jax.random.fold_in(jax.random.fold_in(rng, 6), axis_at), (parts,), jnp.float32, smallest / len(split), top_value / len(split))
        return jnp.repeat(jnp.exp(steps), extent[axis_at] // parts).reshape((-1,) + (1,) * (len(extent) - axis_at - 1))

    loudness = one(*split[0])
    for cut in split[1:]:
        loudness = loudness * one(*cut)
    return loudness


def bell_draw(own_key, shape, spread, reach, split=(), held_as=jnp.bfloat16):
    array = spread * jax.random.normal(own_key, shape, jnp.float32)
    if split:
        array = array * block_levels(own_key, shape, split, -0.22, 0.18)
    return jnp.clip(array, -reach, reach).astype(held_as)


def setup_inputs(seed: int = 0) -> dict:
    key_list = jax.random.split(jax.random.key(seed), 3)
    return {
        "snapshots": bell_draw(key_list[0], (DOF_TOTAL, SNAPSHOTS), 1.0, 6.0, ((0, 16), (1, 16))),
        "modes": bell_draw(key_list[1], (DOF_TOTAL, BASIS_MODES), DOF_TOTAL ** -0.5, 0.015625, ((0, 16),)),
    }


def build_features(current, first, second):
    steps_count = current.shape[1]
    lead = first.shape[0]
    head = current[0:lead].astype(jnp.float32)
    prod_one = (head[:, None, :] * first.astype(jnp.float32)[None, :, :]).reshape(lead * lead, steps_count)
    prod_two = (head[:, None, :] * second.astype(jnp.float32)[None, :, :]).reshape(lead * lead, steps_count)
    return jnp.concatenate([current.astype(jnp.float32), prod_one, prod_two], axis=0).astype(jnp.bfloat16)


def reference(snapshots, modes):
    def project(block_id):
        start = (block_id * SNAP_DEV).astype(jnp.int32)
        piece = lax.dynamic_slice_in_dim(snapshots, start, SNAP_DEV, 1)
        return lax.dot_general(modes, piece, (((0,), (0,)), ((), ())), preferred_element_type=jnp.float32)

    blocks = lax.map(project, jnp.arange(N_TM, dtype=jnp.int32))
    coeffs = jnp.concatenate([blocks[k] for k in range(N_TM)], axis=1).astype(jnp.bfloat16)
    lead = coeffs[0:LEAD_MODES]
    first = jnp.pad(lead, ((0, 0), (DELAY_GAP, 0)))[:, 0:SNAPSHOTS]
    second = jnp.pad(lead, ((0, 0), (2 * DELAY_GAP, 0)))[:, 0:SNAPSHOTS]
    target = jnp.pad(coeffs, ((0, 0), (0, DELAY_GAP)))[:, DELAY_GAP:]
    phi = build_features(coeffs, first, second)
    gram = jnp.dot(phi, phi.T, preferred_element_type=jnp.float32) / SNAPSHOTS + 0.05 * jnp.eye(FEATURES, dtype=jnp.float32)
    rhs = jnp.dot(phi, target.T, preferred_element_type=jnp.float32) / SNAPSHOTS
    return gram, rhs
```

```python
import functools

import jax
import jax.numpy as jnp
from jax import lax
from jax.experimental import pallas as pl
from jax.experimental.pallas import tpu as pltpu
from jax.sharding import PartitionSpec as P

LEAD = 48
RIDGE = 0.05
GROUP = 16
MESH = pl.DeviceIdType.MESH
F32 = jnp.float32
BF16 = jnp.bfloat16


def kernel(
    n, per_block, chunks,
    snaps, modes, gram, rhs_t,
    sbuf, mbuf, psum, part, rsbuf, coef, lead, direct, head, left, right, acc, sib, fin, turned, colbuf, rowbuf,
    load_sem, rs_send, rs_recv, ag_send, ag_recv, g_send, g_recv, sib_send, sib_recv, msg_send, col_recv, row_recv,
):
    s = lax.axis_index("space")
    t = lax.axis_index("tm")
    core = lax.rem(t, 2)
    other = t + 1 - 2 * core
    rows = GROUP * per_block
    span = rows + GROUP
    dof, snap = snaps.shape
    half = snap // 2
    depth = dof // chunks
    total = n * snap
    tile0 = (rows // 128) * 128
    jblocks = LEAD // GROUP

    def loads(c):
        at = pl.ds(pl.multiple_of(c * depth, depth), depth)
        return (
            pltpu.make_async_copy(snaps.at[at, :], sbuf.at[c], load_sem.at[0, c]),
            pltpu.make_async_copy(modes.at[at, :], mbuf.at[c], load_sem.at[1, c]),
        )

    @pl.loop(0, chunks)
    def _(c):
        for copy in loads(c):
            copy.start()

    barrier = pltpu.get_barrier_semaphore()

    @pl.loop(1, n)
    def _(d):
        pl.semaphore_signal(barrier, inc=1, device_id=(lax.rem(s + d, n), t), device_id_type=MESH)
        pl.semaphore_signal(barrier, inc=1, device_id=(s, lax.rem(t + d, n)), device_id_type=MESH)

    psum[...] = jnp.zeros_like(psum)

    @pl.loop(0, chunks)
    def _(c):
        for copy in loads(c):
            copy.wait()
        psum[...] += lax.dot_general(
            mbuf[c], sbuf[c], (((0,), (0,)), ((), ())), preferred_element_type=F32
        )

    part[...] = psum[...].astype(BF16)
    pl.semaphore_wait(barrier, 2 * (n - 1))

    def group(k):
        return pl.ds(pl.multiple_of(k * GROUP, GROUP), GROUP)

    def rs_copy(d):
        peer = lax.rem(s + d, n)
        return pltpu.make_async_remote_copy(
            part.at[group(peer), :], rsbuf.at[s], rs_send.at[d], rs_recv.at[s], device_id=(peer, t), device_id_type=MESH
        )

    def rs_arrival(k):
        return pltpu.make_async_remote_copy(
            part.at[group(k), :], rsbuf.at[k], rs_send.at[0], rs_recv.at[k], device_id=(k, t), device_id_type=MESH
        )

    @pl.loop(1, n)
    def _(d):
        rs_copy(d).start()

    rsbuf[s] = part[group(s), :]

    @pl.loop(1, n)
    def _(d):
        rs_arrival(lax.rem(s + n - d, n)).wait_recv()

    value = psum[group(s), :] - rsbuf[s].astype(F32)
    for k in range(n):
        value = value + rsbuf[k].astype(F32)
    coef[group(s), :] = value.astype(BF16)

    def ag_copy(d):
        peer = lax.rem(s + d, n)
        return pltpu.make_async_remote_copy(
            coef.at[group(s), :], coef.at[group(s), :], ag_send.at[d], ag_recv.at[s], device_id=(peer, t), device_id_type=MESH
        )

    def ag_arrival(k):
        return pltpu.make_async_remote_copy(
            coef.at[group(k), :], coef.at[group(k), :], ag_send.at[0], ag_recv.at[k], device_id=(k, t), device_id_type=MESH
        )

    @pl.loop(1, n)
    def _(d):
        ag_copy(d).start()

    @pl.loop(1, n)
    def _(d):
        ag_arrival(lax.rem(s + n - d, n)).wait_recv()

    def pieces(u):
        c, pair = lax.rem(u, 2), lax.div(u, 2)
        lanes = pl.ds(pl.multiple_of(c * half, half), half)
        return (
            (coef.at[pl.ds(0, LEAD), lanes], lead.at[t + 2, pl.ds(0, LEAD), :]),
            (coef.at[group(s), lanes], lead.at[t + 2, pl.ds(LEAD, GROUP), :]),
            (coef.at[pl.ds(pl.multiple_of(pair * 2 * GROUP, 2 * GROUP), 2 * GROUP), lanes], direct.at[t]),
        )

    def g_copies(d):
        u = lax.rem(t + d, n)
        return [
            pltpu.make_async_remote_copy(src, dst, g_send.at[k, d], g_recv.at[k, t], device_id=(s, u), device_id_type=MESH)
            for k, (src, dst) in enumerate(pieces(u))
        ]

    def g_arrivals(u):
        dsts = (lead.at[u + 2, pl.ds(0, LEAD), :], lead.at[u + 2, pl.ds(LEAD, GROUP), :], direct.at[u])
        return [
            pltpu.make_async_remote_copy(dst, dst, g_send.at[k, 0], g_recv.at[k, u], device_id=(s, u), device_id_type=MESH)
            for k, dst in enumerate(dsts)
        ]

    @pl.loop(1, n)
    def _(d):
        for copy in g_copies(d):
            copy.start()

    lead[0] = jnp.zeros_like(lead[0])
    lead[1] = jnp.zeros_like(lead[1])
    lead[n + 2] = jnp.zeros_like(lead[n + 2])
    mine = pl.ds(pl.multiple_of(core * half, half), half)
    lead[t + 2, 0:LEAD, :] = coef[0:LEAD, mine]
    lead[t + 2, LEAD : LEAD + GROUP, :] = coef[group(s), mine]
    pair = lax.div(t, 2)
    direct[t] = coef[pl.ds(pl.multiple_of(pair * 2 * GROUP, 2 * GROUP), 2 * GROUP), mine]

    @pl.loop(1, n)
    def _(d):
        for copy in g_arrivals(lax.rem(t + n - d, n)):
            copy.wait_recv()

    for tt in range(n):
        head[tt] = lead[tt + 2, 0:LEAD, :].astype(F32)
        at = slice(tt * half, (tt + 1) * half)
        left[rows:span, at] = direct[tt, 0:GROUP, :]
        left[span + rows : 2 * span, at] = direct[tt, GROUP : 2 * GROUP, :]
        right[rows:span, at] = lead[tt + 3, LEAD : LEAD + GROUP, :]
        right[span : span + GROUP, at] = lead[tt + 2, LEAD : LEAD + GROUP, :]

    products = LEAD * jblocks

    def features(dst, base, block):
        @pl.loop(0, per_block)
        def _(k):
            q = jnp.maximum(block * per_block + k - n, 0)
            later = lax.div(q, products)
            q = q - later * products
            i, jb = lax.div(q, jblocks), lax.rem(q, jblocks)
            for tt in range(n):
                delayed = lead[tt + 1 - later, group(jb), :].astype(F32)
                row = head[tt, pl.ds(i, 1), :]
                at = pl.ds(pl.multiple_of(base + k * GROUP, GROUP), GROUP)
                dst[at, tt * half : (tt + 1) * half] = (row * delayed).astype(BF16)

    features(left, 0, 2 * pair)
    features(left, span, 2 * pair + 1)
    features(right, 0, s)

    acc[...] = jnp.zeros_like(acc)
    wide = 4 * half

    @pl.loop(0, n // 4)
    def _(c):
        at = pl.ds(pl.multiple_of(c * wide, wide), wide)
        acc[:, 0 : span + GROUP] += lax.dot_general(
            left[:, at], right[:, at], (((1,), (1,)), ((), ())), preferred_element_type=F32
        )

    swap = pltpu.make_async_remote_copy(
        acc.at[pl.ds(pl.multiple_of((1 - core) * span, GROUP), span), :], sib, sib_send, sib_recv,
        device_id=(s, other), device_id_type=MESH,
    )
    swap.start()
    fin[...] = jnp.zeros_like(fin)
    swap.wait()
    fin[0:span, :] = acc[pl.ds(pl.multiple_of(core * span, GROUP), span), :] + sib[...]

    turned[...] = fin[:, tile0 : tile0 + 128].T
    first = span - tile0
    col_msg = turned.at[pl.ds(first, GROUP), :]

    @pl.when(s != 0)
    def _():
        copy = pltpu.make_async_remote_copy(
            col_msg, colbuf.at[group(s), :], msg_send.at[0], col_recv.at[s], device_id=(0, t), device_id_type=MESH
        )
        copy.start()
        copy.wait_send()

    @pl.when(s == 0)
    def _():
        colbuf[0:GROUP, :] = turned[first : first + GROUP, :]

        @pl.loop(1, n)
        def _(k):
            pltpu.make_async_remote_copy(
                col_msg, colbuf.at[group(k), :], msg_send.at[0], col_recv.at[k], device_id=(k, t), device_id_type=MESH
            ).wait_recv()

        fin[:, 0 : n * GROUP] = colbuf[...].T[:, 0 : n * GROUP]

    row_msg = fin.at[pl.ds(rows, GROUP), :]

    @pl.when(t != 0)
    def _():
        copy = pltpu.make_async_remote_copy(
            row_msg, rowbuf.at[group(t), :], msg_send.at[1], row_recv.at[t], device_id=(s, 0), device_id_type=MESH
        )
        copy.start()
        copy.wait_send()

    @pl.when(t == 0)
    def _():
        rowbuf[0:GROUP, :] = fin[rows:span, :]

        @pl.loop(1, n)
        def _(k):
            pltpu.make_async_remote_copy(
                row_msg, rowbuf.at[group(k), :], msg_send.at[1], row_recv.at[k], device_id=(s, k), device_id_type=MESH
            ).wait_recv()

        fin[0 : n * GROUP, :] = rowbuf[0 : n * GROUP, :]

    turned[...] = fin[:, tile0 : tile0 + 128].T
    scale = 1.0 / total
    rhs_t[...] = turned[rows - tile0 : span - tile0, 0:rows] * scale
    delta = s * rows - t * rows
    on_diagonal = (
        lax.broadcasted_iota(jnp.int32, (rows, rows), 0) == lax.broadcasted_iota(jnp.int32, (rows, rows), 1) + delta
    )
    gram[...] = fin[0:rows, 0:rows] * scale + jnp.where(on_diagonal, RIDGE, 0.0)

    @pl.loop(1, n)
    def _(d):
        rs_copy(d).wait_send()
        ag_copy(d).wait_send()
        for copy in g_copies(d):
            copy.wait_send()


def per_device(snapshots, modes, *, n):
    dof, snap = snapshots.shape
    count = modes.shape[1]
    assert count == n * GROUP
    features = count + 2 * LEAD * LEAD
    rows = features // n
    span = rows + GROUP
    tall = -(-(span + GROUP) // 128) * 128
    half = snap // 2
    chunks = 10 if dof % 2560 == 0 else 2
    depth = dof // chunks
    dma, vmem = pltpu.SemaphoreType.DMA, pltpu.VMEM
    gram, rhs_t = pl.pallas_call(
        functools.partial(kernel, n, rows // GROUP, chunks),
        out_shape=(
            jax.ShapeDtypeStruct((rows, rows), F32),
            jax.ShapeDtypeStruct((GROUP, rows), F32),
        ),
        in_specs=[pl.BlockSpec(memory_space=pl.ANY)] * 2,
        out_specs=(pl.BlockSpec(memory_space=pltpu.VMEM),) * 2,
        scratch_shapes=[
            vmem((chunks, depth, snap), BF16),
            vmem((chunks, depth, count), BF16),
            vmem((count, snap), F32),
            vmem((count, snap), BF16),
            vmem((n, GROUP, snap), BF16),
            vmem((count, snap), BF16),
            vmem((n + 3, LEAD + GROUP, half), BF16),
            vmem((n, 2 * GROUP, half), BF16),
            vmem((n, LEAD, half), F32),
            vmem((2 * span, n * half), BF16),
            vmem((span + GROUP, n * half), BF16),
            vmem((2 * span, tall), F32),
            vmem((span, tall), F32),
            vmem((tall, tall), F32),
            vmem((128, tall), F32),
            vmem((max(n * GROUP, 128), tall), F32),
            vmem((n * GROUP, tall), F32),
            dma((2, chunks)),
            dma((n,)), dma((n,)), dma((n,)), dma((n,)),
            dma((3, n)), dma((3, n)),
            dma, dma, dma((2,)), dma((n,)), dma((n,)),
        ],
        compiler_params=pltpu.CompilerParams(
            collective_id=0, has_side_effects=True, vmem_limit_bytes=60 * 1024 * 1024
        ),
    )(snapshots, modes)
    return gram, rhs_t.T


def solution(mesh):
    n = mesh.shape["tm"]
    assert mesh.shape["space"] == n
    return jax.shard_map(
        functools.partial(per_device, n=n),
        mesh=mesh,
        in_specs=(P("space", "tm"), P("space", None)),
        out_specs=(P("tm", "space"), P("tm", "space")),
        check_vma=False,
    )
```

```python
import functools

import jax
import jax.numpy as jnp
from jax import lax
from jax.experimental import pallas as pl
from jax.experimental.pallas import tpu as pltpu
from jax.sharding import PartitionSpec as P

LEAD = 48
RIDGE = 0.05
GROUP = 16
MESH = pl.DeviceIdType.MESH
F32 = jnp.float32
BF16 = jnp.bfloat16


def kernel(
    n, per_block, chunks,
    snaps, modes, gram, rhs_t,
    sbuf, mbuf, mturn, psum, part, rsbuf, coef, stage, lead, direct, head, left, right,
    acc_a, acc_b, sib_a, sib_b, fin, turned, colmsg, rowmsg, colbuf, rowbuf,
    load_sem, rs_send, rs_recv, ag_send, ag_recv, g_send, g_recv, sib_send, sib_recv, msg_send, col_recv, row_recv,
):
    s = lax.axis_index("space")
    t = lax.axis_index("tm")
    core = lax.rem(t, 2)
    other = t + 1 - 2 * core
    pair = lax.div(t, 2)
    rows = GROUP * per_block
    span = rows + GROUP
    dof, snap = snaps.shape
    half, lanes = snap // 2, snap // 4
    depth = dof // chunks
    total = n * snap
    tile0 = (rows // 128) * 128
    jblocks = LEAD // GROUP

    def group(k):
        return pl.ds(pl.multiple_of(k * GROUP, GROUP), GROUP)

    def loads(c, h):
        at = pl.ds(pl.multiple_of(c * depth, depth), depth)
        copies = [
            pltpu.make_async_copy(
                snaps.at[at, pl.ds(k * half + h * lanes, lanes)],
                sbuf.at[h, c, :, pl.ds(k * lanes, lanes)],
                load_sem.at[2 * h + k, c],
            )
            for k in range(2)
        ]
        if h == 0:
            copies.append(pltpu.make_async_copy(modes.at[at, :], mbuf.at[c], load_sem.at[4, c]))
        return copies

    for h in range(2):

        @pl.loop(0, chunks)
        def _(c):
            for copy in loads(c, h):
                copy.start()

    barrier = pltpu.get_barrier_semaphore()

    @pl.loop(1, n)
    def _(d):
        pl.semaphore_signal(barrier, inc=1, device_id=(lax.rem(s + d, n), t), device_id_type=MESH)
        pl.semaphore_signal(barrier, inc=1, device_id=(s, lax.rem(t + d, n)), device_id_type=MESH)

    def rs_copy(h, d):
        peer = lax.rem(s + d, n)
        return pltpu.make_async_remote_copy(
            part.at[h, group(peer), :], rsbuf.at[h, s], rs_send.at[h, d], rs_recv.at[h, s],
            device_id=(peer, t), device_id_type=MESH,
        )

    def rs_arrival(h, k):
        return pltpu.make_async_remote_copy(
            part.at[h, group(k), :], rsbuf.at[h, k], rs_send.at[h, 0], rs_recv.at[h, k],
            device_id=(k, t), device_id_type=MESH,
        )

    def ag_copy(h, d):
        return pltpu.make_async_remote_copy(
            coef.at[h, group(s), :], coef.at[h, group(s), :], ag_send.at[h, d], ag_recv.at[h, s],
            device_id=(lax.rem(s + d, n), t), device_id_type=MESH,
        )

    def ag_arrival(h, k):
        return pltpu.make_async_remote_copy(
            coef.at[h, group(k), :], coef.at[h, group(k), :], ag_send.at[h, 0], ag_recv.at[h, k],
            device_id=(k, t), device_id_type=MESH,
        )

    def pair_rows(which):
        return pl.ds(pl.multiple_of(which * 2 * GROUP, 2 * GROUP), 2 * GROUP)

    def core_lanes(c):
        return pl.ds(pl.multiple_of(c * lanes, lanes), lanes)

    def g_copies(h, d):
        u = lax.rem(t + d, n)
        c = lax.rem(u, 2)
        ends = (
            (stage.at[h, c], lead.at[h, t + 2]),
            (coef.at[h, pair_rows(lax.div(u, 2)), core_lanes(c)], direct.at[h, t]),
        )
        return [
            pltpu.make_async_remote_copy(
                src, dst, g_send.at[h, k, d], g_recv.at[h, k, t], device_id=(s, u), device_id_type=MESH
            )
            for k, (src, dst) in enumerate(ends)
        ]

    def g_arrivals(h, u):
        return [
            pltpu.make_async_remote_copy(
                dst, dst, g_send.at[h, k, 0], g_recv.at[h, k, u], device_id=(s, u), device_id_type=MESH
            )
            for k, dst in enumerate((lead.at[h, u + 2], direct.at[h, u]))
        ]

    def start_rs(h):
        part[h] = psum[h].astype(BF16)
        if h == 0:
            pl.semaphore_wait(barrier, 2 * (n - 1))

        @pl.loop(1, n)
        def _(d):
            rs_copy(h, d).start()

        rsbuf[h, s] = part[h, group(s), :]

    def start_ag(h):
        @pl.loop(1, n)
        def _(d):
            rs_arrival(h, lax.rem(s + n - d, n)).wait_recv()

        value = psum[h, group(s), :] - rsbuf[h, s].astype(F32)
        for k in range(n):
            value = value + rsbuf[h, k].astype(F32)
        coef[h, group(s), :] = value.astype(BF16)

        @pl.loop(1, n)
        def _(d):
            ag_copy(h, d).start()

    def start_gather(h):
        @pl.loop(1, n)
        def _(d):
            ag_arrival(h, lax.rem(s + n - d, n)).wait_recv()

        for c in range(2):
            stage[h, c, 0:LEAD, :] = coef[h, 0:LEAD, c * lanes : (c + 1) * lanes]
            stage[h, c, LEAD : LEAD + GROUP, :] = coef[h, group(s), c * lanes : (c + 1) * lanes]

        @pl.loop(1, n)
        def _(d):
            for copy in g_copies(h, d):
                copy.start()

        lead[h, t + 2] = stage[h, core]
        direct[h, t] = coef[h, pair_rows(pair), core_lanes(core)]

    products = LEAD * jblocks

    def features(h, dst, base, block):
        @pl.loop(0, per_block)
        def _(k):
            q = jnp.maximum(block * per_block + k - n, 0)
            later = lax.div(q, products)
            q = q - later * products
            i, jb = lax.div(q, jblocks), lax.rem(q, jblocks)
            at = pl.ds(pl.multiple_of(base + k * GROUP, GROUP), GROUP)
            for tt in range(n):
                delayed = lead[h, tt + 1 - later, group(jb), :].astype(F32)
                row = head[tt, pl.ds(i, 1), :]
                dst[h, at, tt * lanes : (tt + 1) * lanes] = (row * delayed).astype(BF16)

    def build(h):
        @pl.loop(1, n)
        def _(d):
            for copy in g_arrivals(h, lax.rem(t + n - d, n)):
                copy.wait_recv()

        for tt in range(n):
            head[tt] = lead[h, tt + 2, 0:LEAD, :].astype(F32)
            at = slice(tt * lanes, (tt + 1) * lanes)
            left[h, rows:span, at] = direct[h, tt, 0:GROUP, :]
            left[h, span + rows : 2 * span, at] = direct[h, tt, GROUP : 2 * GROUP, :]
            right[h, rows:span, at] = lead[h, tt + 3, LEAD : LEAD + GROUP, :]
            right[h, span : span + GROUP, at] = lead[h, tt + 2, LEAD : LEAD + GROUP, :]
        features(h, right, 0, s)
        features(h, left, 0, 2 * pair)
        features(h, left, span, 2 * pair + 1)

    def contract(a, b):
        return lax.dot_general(a, b, (((1,), (1,)), ((), ())), preferred_element_type=F32)

    for h in range(2):
        psum[h] = jnp.zeros_like(psum[h])

        @pl.loop(0, chunks)
        def _(c):
            for copy in loads(c, h):
                copy.wait()
            if h == 0:
                across = mbuf[c].T
                mturn[c] = across
            else:
                across = mturn[c]
            psum[h] += jnp.dot(across, sbuf[h, c], preferred_element_type=F32)

        start_rs(h)

    for h in range(2):
        lead[h, 0] = jnp.zeros_like(lead[h, 0])
        lead[h, 1] = jnp.zeros_like(lead[h, 1])
        lead[h, n + 2] = jnp.zeros_like(lead[h, n + 2])
    fin[...] = jnp.zeros_like(fin)
    acc_b[...] = jnp.zeros_like(acc_b)
    start_ag(0)
    start_ag(1)
    start_gather(0)
    start_gather(1)

    end = span + GROUP
    build(0)
    acc_b[:, 0 : end - tile0] = contract(left[0], right[0, tile0:end, :])
    acc_a[...] = contract(left[0], right[0, 0:tile0, :])
    build(1)
    acc_b[:, 0 : end - tile0] += contract(left[1], right[1, tile0:end, :])

    theirs = pl.ds(pl.multiple_of((1 - core) * span, GROUP), span)
    ours = pl.ds(pl.multiple_of(core * span, GROUP), span)

    def swap(k, acc, sib):
        return pltpu.make_async_remote_copy(
            acc.at[theirs, :], sib, sib_send.at[k], sib_recv.at[k], device_id=(s, other), device_id_type=MESH
        )

    swap_b, swap_a = swap(0, acc_b, sib_b), swap(1, acc_a, sib_a)
    swap_b.start()
    acc_a[theirs, :] += contract(left[1, theirs, :], right[1, 0:tile0, :])
    swap_a.start()
    swap_b.wait()
    fin[0:span, tile0 : tile0 + 128] = acc_b[ours, :] + sib_b[...]

    turned[...] = fin[:, tile0 : tile0 + 128].T
    first = span - tile0
    colmsg[...] = turned[first : first + GROUP, :].astype(BF16)

    def col_copy(k, peer):
        return pltpu.make_async_remote_copy(
            colmsg, colbuf.at[group(k), :], msg_send.at[0], col_recv.at[k], device_id=(peer, t), device_id_type=MESH
        )

    @pl.when(s != 0)
    def _():
        col_copy(s, 0).start()

    acc_a[ours, :] += contract(left[1, ours, :], right[1, 0:tile0, :])
    swap_a.wait()
    fin[0:span, 0:tile0] = acc_a[ours, :] + sib_a[...]

    @pl.when(s != 0)
    def _():
        col_copy(s, 0).wait_send()

    @pl.when(s == 0)
    def _():
        colbuf[0:GROUP, :] = colmsg[...]

        @pl.loop(1, n)
        def _(k):
            col_copy(k, k).wait_recv()

        fin[:, 0 : n * GROUP] = colbuf[...].astype(F32).T[:, 0 : n * GROUP]

    def row_copy(k, peer):
        return pltpu.make_async_remote_copy(
            rowmsg, rowbuf.at[group(k), :], msg_send.at[1], row_recv.at[k], device_id=(s, peer), device_id_type=MESH
        )

    rowmsg[...] = fin[rows:span, :].astype(BF16)

    @pl.when(t != 0)
    def _():
        row_copy(t, 0).start()

    @pl.when(t == 0)
    def _():
        rowbuf[0:GROUP, :] = rowmsg[...]

        @pl.loop(1, n)
        def _(k):
            row_copy(k, k).wait_recv()

        fin[0 : n * GROUP, :] = rowbuf[...].astype(F32)

    turned[...] = fin[:, tile0 : tile0 + 128].T
    scale = 1.0 / total
    rhs_t[...] = turned[rows - tile0 : span - tile0, 0:rows] * scale
    delta = s * rows - t * rows
    on_diagonal = (
        lax.broadcasted_iota(jnp.int32, (rows, rows), 0) == lax.broadcasted_iota(jnp.int32, (rows, rows), 1) + delta
    )
    gram[...] = fin[0:rows, 0:rows] * scale + jnp.where(on_diagonal, RIDGE, 0.0)

    @pl.when(t != 0)
    def _():
        row_copy(t, 0).wait_send()

    for h in range(2):

        @pl.loop(1, n)
        def _(d):
            rs_copy(h, d).wait_send()
            ag_copy(h, d).wait_send()
            for copy in g_copies(h, d):
                copy.wait_send()


def per_device(snapshots, modes, *, n):
    dof, snap = snapshots.shape
    count = modes.shape[1]
    assert count == n * GROUP
    features = count + 2 * LEAD * LEAD
    rows = features // n
    span = rows + GROUP
    tile0 = rows // 128 * 128
    tall = tile0 + 128
    assert span + GROUP <= tall
    half, lanes = snap // 2, snap // 4
    chunks = 10 if dof % 2560 == 0 else 2
    depth = dof // chunks
    dma, vmem = pltpu.SemaphoreType.DMA, pltpu.VMEM
    gram, rhs_t = pl.pallas_call(
        functools.partial(kernel, n, rows // GROUP, chunks),
        out_shape=(
            jax.ShapeDtypeStruct((rows, rows), F32),
            jax.ShapeDtypeStruct((GROUP, rows), F32),
        ),
        in_specs=[pl.BlockSpec(memory_space=pl.ANY)] * 2,
        out_specs=(pl.BlockSpec(memory_space=pltpu.VMEM),) * 2,
        scratch_shapes=[
            vmem((2, chunks, depth, half), BF16),
            vmem((chunks, depth, count), BF16),
            vmem((chunks, count, depth), BF16),
            vmem((2, count, half), F32),
            vmem((2, count, half), BF16),
            vmem((2, n, GROUP, half), BF16),
            vmem((2, count, half), BF16),
            vmem((2, 2, LEAD + GROUP, lanes), BF16),
            vmem((2, n + 3, LEAD + GROUP, lanes), BF16),
            vmem((2, n, 2 * GROUP, lanes), BF16),
            vmem((n, LEAD, lanes), F32),
            vmem((2, 2 * span, n * lanes), BF16),
            vmem((2, span + GROUP, n * lanes), BF16),
            vmem((2 * span, tile0), F32),
            vmem((2 * span, 128), F32),
            vmem((span, tile0), F32),
            vmem((span, 128), F32),
            vmem((tall, tall), F32),
            vmem((128, tall), F32),
            vmem((GROUP, tall), BF16),
            vmem((GROUP, tall), BF16),
            vmem((max(n * GROUP, 128), tall), BF16),
            vmem((n * GROUP, tall), BF16),
            dma((5, chunks)),
            dma((2, n)), dma((2, n)), dma((2, n)), dma((2, n)),
            dma((2, 2, n)), dma((2, 2, n)),
            dma((2,)), dma((2,)), dma((2,)), dma((n,)), dma((n,)),
        ],
        compiler_params=pltpu.CompilerParams(
            collective_id=0, has_side_effects=True, vmem_limit_bytes=51 * 1024 * 1024
        ),
    )(snapshots, modes)
    return gram, rhs_t.T


def solution(mesh):
    n = mesh.shape["tm"]
    assert mesh.shape["space"] == n
    return jax.shard_map(
        functools.partial(per_device, n=n),
        mesh=mesh,
        in_specs=(P("space", "tm"), P("space", None)),
        out_specs=(P("tm", "space"), P("tm", "space")),
        check_vma=False,
    )
```
